256 devices in a mesh: frame: 64 (over y, z, core), text: 4 (over x).
Axes of the slice: x: 4, y: 4, z: 8, core: 2. Of those that a mesh axis runs over, the one named last changes fastest.
Arguments:
- frame_keys: bfloat16 [32768, 4096], P('frame', 'text'), may hold values from -6 to 6
- frame_values: bfloat16 [32768, 4096], P('frame', 'text'), may hold values from -6 to 6
- frame_grads: bfloat16 [32768, 4096], P('frame', 'text'), may hold values from -6 to 6
- text_keys: bfloat16 [8192, 4096], P(('frame', 'text')), may hold values from -6 to 6
- text_values: bfloat16 [8192, 4096], P(('frame', 'text')), may hold values from -6 to 6
- text_grads: bfloat16 [8192, 4096], P(('frame', 'text')), may hold values from -6 to 6
- band_first: int32 [256], P('frame'), may hold values from 0 to 63, as said below
- band_count: int32 [256], P('frame'), may hold values from 1 to 3
Outputs:
- frame_out: bfloat16 [32768, 4096], P('frame', 'text')
- text_out: bfloat16 [8192, 4096], P('frame', 'text')
- frame_key_grad: bfloat16 [32768, 4096], P('frame', 'text')
- frame_value_grad: bfloat16 [32768, 4096], P('frame', 'text')
- text_key_grad: bfloat16 [8192, 4096], P('frame', 'text')
- text_value_grad: bfloat16 [8192, 4096], P('frame', 'text')
The draws below stay inside these ranges and needn't reach their ends.
Inputs may be any that keep to these rules, and one draw needn't show every extreme that they name: For frame block b, band_first[b] is b // 4 - 1 or b // 4, and band_first[b] + band_count[b] - 1 is b // 4 or b // 4 + 1, so every text block lies in some band.
All inputs are finite; a program needn't handle non-finite values.
Results may differ from the reference program's by a relative error of at most 0.023.
Values may be sent and summed in bfloat16 or wider, within the bound.
A program may use at most 128 MiB of HBM per device.

```python
import math
import jax
import jax.numpy as jnp
from jax import lax

HEADS = 32
HEAD_DIM = 128
BLOCK = 128
FRAME_DEV = 512
TOKENS = 8192
FRAMES = 32768


def draw_keys(key, rows_all, frame_side):
    sample = jax.random.truncated_normal(jax.random.fold_in(key, 11 + frame_side), -6.0, 6.0, (rows_all, HEADS * HEAD_DIM), jnp.float32)
    return sample.astype(jnp.bfloat16)


def draw_frame_keys(key, part):
    return draw_keys(key, FRAMES, 1)


def draw_text_keys(key, part):
    return draw_keys(key, TOKENS, 0)


def band_table(key):
    frame_blocks = FRAMES // BLOCK
    text_blocks = TOKENS // BLOCK
    per_device = FRAME_DEV // BLOCK
    centre = jnp.arange(frame_blocks, dtype=jnp.int32) // 4
    speed = jax.random.randint(jax.random.fold_in(key, 7), (frame_blocks // per_device,), 0, 2)
    chance = jnp.repeat(jnp.where(speed == 1, 17, 3), per_device)
    back_draw = jax.random.randint(jax.random.fold_in(key, 8), (frame_blocks,), 0, 20) < chance
    ahead_draw = jax.random.randint(jax.random.fold_in(key, 9), (frame_blocks,), 0, 20) < chance
    backward = jnp.where(back_draw & (centre > 0), 1, 0)
    forward = jnp.where(ahead_draw & (centre < text_blocks - 1), 1, 0)
    forced = jnp.arange(frame_blocks, dtype=jnp.int32) == 4
    backward = jnp.where(forced, 1, backward)
    forward = jnp.where(forced, 1, forward)
    return ((centre - backward).astype(jnp.int32), (1 + backward + forward).astype(jnp.int32))


def draw_band_first(key, part):
    return band_table(key)[0]


def draw_band_count(key, part):
    return band_table(key)[1]


def level_of(own_key, shape, cuts, smallest, largest):
    def one(position, blocks):
        steps = jax.random.uniform(jax.random.fold_in(jax.random.fold_in(own_key, 6), position), (blocks,), jnp.float32, smallest / len(cuts), largest / len(cuts))
        return jnp.repeat(jnp.exp(steps), shape[position] // blocks).reshape((-1,) + (1,) * (len(shape) - position - 1))

    gain = one(*cuts[0])
    for cut in cuts[1:]:
        gain = gain * one(*cut)
    return gain


def centred(key, extent, spread, limit, split=(), held_as=jnp.bfloat16):
    entries = jax.random.normal(key, extent, jnp.float32) * spread
    if len(split) > 0:
        entries = level_of(key, extent, split, -0.22, 0.18) * entries
    return jnp.clip(entries, min=-limit, max=limit).astype(held_as)


def setup_inputs(seed: int = 0) -> dict:
    splits = jax.random.split(jax.random.key(seed), 9)
    return {
        "frame_keys": draw_frame_keys(jax.random.fold_in(splits[8], 71), 0),
        "frame_values": centred(splits[1], (FRAMES, HEADS * HEAD_DIM), 1.0, 6.0, ((0, 64), (1, 4))),
        "frame_grads": centred(splits[2], (FRAMES, HEADS * HEAD_DIM), 1.0, 6.0, ((0, 64), (1, 4))),
        "text_keys": draw_text_keys(jax.random.fold_in(splits[8], 71), 0),
        "text_values": centred(splits[4], (TOKENS, HEADS * HEAD_DIM), 1.0, 6.0, ((0, 256),)),
        "text_grads": centred(splits[5], (TOKENS, HEADS * HEAD_DIM), 1.0, 6.0, ((0, 256),)),
        "band_first": draw_band_first(jax.random.fold_in(splits[8], 71), 0),
        "band_count": draw_band_count(jax.random.fold_in(splits[8], 71), 0),
    }


NEGATIVE = -1e+30

def live_blocks(first_ids, count_ids, text_ids):
    lower = first_ids[:, None]
    upper = lower + count_ids[:, None]
    return (text_ids[None, :] >= lower) & (text_ids[None, :] < upper)

def widen_mask(inside):
    row_blocks, col_blocks = inside.shape
    grown = jnp.broadcast_to(inside[:, None, :, None], (row_blocks, BLOCK, col_blocks, BLOCK))
    return grown.reshape(row_blocks * BLOCK, col_blocks * BLOCK)

def padded(source, before, after, filler):
    shape_rest = source.shape[1:]
    leading = jnp.full((before,) + shape_rest, filler, source.dtype)
    trailing = jnp.full((after,) + shape_rest, filler, source.dtype)
    return jnp.concatenate([leading, source, trailing], axis=0)

def low_then_high(source):
    return lax.optimization_barrier(source.astype(jnp.bfloat16)).astype(jnp.float32)

def reference(frame_keys, frame_values, frame_grads, text_keys, text_values, text_grads, band_first, band_count):
    score_scale = 1.0 / math.sqrt(HEAD_DIM)
    frame_blocks = FRAMES // BLOCK
    text_blocks = TOKENS // BLOCK

    def split_frames(source):
        return source.reshape(frame_blocks, BLOCK, HEADS, HEAD_DIM)

    def split_text(source):
        return source.reshape(text_blocks, BLOCK, HEADS, HEAD_DIM)
    frame_key_blocks = split_frames(frame_keys)
    frame_value_blocks = split_frames(frame_values)
    frame_grad_blocks = split_frames(frame_grads)
    text_key_blocks = split_text(text_keys)
    text_value_blocks = split_text(text_values)
    text_grad_blocks = split_text(text_grads)
    text_key_pad = padded(text_key_blocks, 1, 1, 0.0)
    text_value_pad = padded(text_value_blocks, 1, 1, 0.0)
    text_grad_pad = padded(text_grad_blocks, 1, 1, 0.0)

    def text_window(source, centre):
        return lax.dynamic_slice_in_dim(source, centre, 3, 0).reshape(3 * BLOCK, HEADS, HEAD_DIM).astype(jnp.float32)

    def frame_mask(block_id, centre):
        text_ids = centre - 1 + jnp.arange(3, dtype=jnp.int32)
        return widen_mask(live_blocks(band_first[block_id][None], band_count[block_id][None], text_ids))

    def frame_side(block_id):
        centre = block_id // 4
        keys_win = text_window(text_key_pad, centre)
        values_win = text_window(text_value_pad, centre)
        own_keys = frame_key_blocks[block_id].astype(jnp.float32)
        own_grads = frame_grad_blocks[block_id].astype(jnp.float32)
        scores = score_scale * jnp.einsum('fhd,thd->hft', own_keys, keys_win)
        live_pairs = frame_mask(block_id, centre)[None]
        row_max = lax.optimization_barrier(jnp.max(jnp.where(live_pairs, scores, NEGATIVE), axis=2))
        row_exp = jnp.exp(jnp.where(live_pairs, scores - row_max[:, :, None], NEGATIVE))
        row_total = lax.optimization_barrier(jnp.sum(row_exp, axis=2))
        row_low = low_then_high(row_exp / row_total[:, :, None])
        frame_out = jnp.einsum('hft,thd->fhd', row_low, values_win).astype(jnp.bfloat16)
        frame_dot = lax.optimization_barrier(jnp.sum(own_grads * frame_out.astype(jnp.float32), axis=2)).T
        return (row_max, row_total, frame_out, frame_dot)
    row_max_all, row_total_all, frame_out_all, frame_dot_all = lax.map(frame_side, jnp.arange(frame_blocks, dtype=jnp.int32))
    frame_key_pad = padded(frame_key_blocks, 4, 4, 0.0)
    frame_value_pad = padded(frame_value_blocks, 4, 4, 0.0)
    frame_grad_pad = padded(frame_grad_blocks, 4, 4, 0.0)
    row_max_pad = padded(row_max_all, 4, 4, 0.0)
    row_total_pad = padded(row_total_all, 4, 4, 1.0)
    frame_dot_pad = padded(frame_dot_all, 4, 4, 0.0)
    first_pad = padded(band_first, 4, 4, 0)
    count_pad = padded(band_count, 4, 4, 0)

    def frames_window(source, window_start):
        return lax.dynamic_slice_in_dim(source, window_start, 12, 0)

    def rows_of(source, window_start):
        return frames_window(source, window_start).reshape(12 * BLOCK, HEADS, HEAD_DIM).astype(jnp.float32)

    def stats_of(source, window_start):
        return frames_window(source, window_start).transpose(1, 0, 2).reshape(HEADS, 12 * BLOCK)

    def text_side(centre):
        window_start = 4 * centre
        keys_win = rows_of(frame_key_pad, window_start)
        values_win = rows_of(frame_value_pad, window_start)
        grads_win = rows_of(frame_grad_pad, window_start)
        max_win = stats_of(row_max_pad, window_start)
        total_win = stats_of(row_total_pad, window_start)
        dot_win = stats_of(frame_dot_pad, window_start)
        first_win = frames_window(first_pad, window_start)
        count_win = frames_window(count_pad, window_start)
        own_keys = text_key_blocks[centre].astype(jnp.float32)
        own_values = text_value_blocks[centre].astype(jnp.float32)
        own_grads = text_grad_blocks[centre].astype(jnp.float32)
        scores = score_scale * jnp.einsum('fhd,thd->hft', keys_win, own_keys)
        live_pairs = widen_mask(live_blocks(first_win, count_win, centre[None]))[None]
        col_max = lax.optimization_barrier(jnp.max(jnp.where(live_pairs, scores, NEGATIVE), axis=1))
        col_exp = jnp.exp(jnp.where(live_pairs, scores - col_max[:, None, :], NEGATIVE))
        col_total = lax.optimization_barrier(jnp.sum(col_exp, axis=1))
        weighted = jnp.einsum('hft,fhd->thd', low_then_high(col_exp), values_win, precision=lax.Precision.HIGHEST)
        text_out = (weighted / col_total.T[:, :, None]).astype(jnp.bfloat16)
        text_dot = lax.optimization_barrier(jnp.sum(own_grads * text_out.astype(jnp.float32), axis=2)).T
        col_probs = col_exp / col_total[:, None, :]
        row_probs = jnp.exp(jnp.where(live_pairs, scores - max_win[:, :, None], NEGATIVE)) / total_win[:, :, None]
        grad_rows = jnp.einsum('fhd,thd->hft', grads_win, own_values)
        grad_cols = jnp.einsum('fhd,thd->hft', values_win, own_grads)
        grad_score = low_then_high(row_probs * (grad_rows - dot_win[:, :, None]) + col_probs * (grad_cols - text_dot[:, None, :]))
        key_grad = (score_scale * jnp.einsum('hft,fhd->thd', grad_score, keys_win)).astype(jnp.bfloat16)
        value_grad = jnp.einsum('hft,fhd->thd', low_then_high(row_probs), grads_win).astype(jnp.bfloat16)
        return (col_max, col_total, text_dot, text_out, key_grad, value_grad)
    col_max_all, col_total_all, text_dot_all, text_out_all, text_key_all, text_value_all = lax.map(text_side, jnp.arange(text_blocks, dtype=jnp.int32))
    col_max_pad = padded(col_max_all, 1, 1, 0.0)
    col_total_pad = padded(col_total_all, 1, 1, 1.0)
    text_dot_pad = padded(text_dot_all, 1, 1, 0.0)

    def stats_window(source, centre):
        return lax.dynamic_slice_in_dim(source, centre, 3, 0).transpose(1, 0, 2).reshape(HEADS, 3 * BLOCK)

    def frame_back(block_id):
        centre = block_id // 4
        keys_win = text_window(text_key_pad, centre)
        values_win = text_window(text_value_pad, centre)
        grads_win = text_window(text_grad_pad, centre)
        win_max = stats_window(col_max_pad, centre)
        win_total = stats_window(col_total_pad, centre)
        win_dot = stats_window(text_dot_pad, centre)
        own_keys = frame_key_blocks[block_id].astype(jnp.float32)
        own_values = frame_value_blocks[block_id].astype(jnp.float32)
        own_grads = frame_grad_blocks[block_id].astype(jnp.float32)
        scores = score_scale * jnp.einsum('fhd,thd->hft', own_keys, keys_win)
        live_pairs = frame_mask(block_id, centre)[None]
        row_probs = jnp.exp(jnp.where(live_pairs, scores - row_max_all[block_id][:, :, None], NEGATIVE)) / row_total_all[block_id][:, :, None]
        col_probs = jnp.exp(jnp.where(live_pairs, scores - win_max[:, None, :], NEGATIVE)) / win_total[:, None, :]
        grad_rows = jnp.einsum('fhd,thd->hft', own_grads, values_win)
        grad_cols = jnp.einsum('fhd,thd->hft', own_values, grads_win)
        grad_score = low_then_high(row_probs * (grad_rows - frame_dot_all[block_id][:, :, None]) + col_probs * (grad_cols - win_dot[:, None, :]))
        key_grad = (score_scale * jnp.einsum('hft,thd->fhd', grad_score, keys_win)).astype(jnp.bfloat16)
        value_grad = jnp.einsum('hft,thd->fhd', low_then_high(col_probs), grads_win).astype(jnp.bfloat16)
        return (key_grad, value_grad)
    frame_key_all, frame_value_all = lax.map(frame_back, jnp.arange(frame_blocks, dtype=jnp.int32))
    frame_width = HEADS * HEAD_DIM
    return (frame_out_all.reshape(FRAMES, frame_width), text_out_all.reshape(TOKENS, frame_width), frame_key_all.reshape(FRAMES, frame_width), frame_value_all.reshape(FRAMES, frame_width), text_key_all.reshape(TOKENS, frame_width), text_value_all.reshape(TOKENS, frame_width))
```

```python
import functools
import math

import jax
import jax.numpy as jnp
from jax import lax
from jax.experimental import pallas as pl
from jax.experimental.pallas import tpu as pltpu
from jax.sharding import PartitionSpec as P

D = 128
BLOCK = 128
NEGATIVE = -1e30
FLOOR = -1e20
LAG = 2
AHEAD = 4
MESH = pl.DeviceIdType.MESH
F32 = jnp.float32
BF16 = jnp.bfloat16


def dot_nt(a, b):
    return lax.dot_general(a, b, (((1,), (1,)), ((), ())), preferred_element_type=F32)


def dot_nn(a, b):
    return lax.dot_general(a, b, (((1,), (0,)), ((), ())), preferred_element_type=F32)


def dot_tn(a, b):
    return lax.dot_general(a, b, (((0,), (0,)), ((), ())), preferred_element_type=F32)


def kernel(
    fdim, tdim, heads,
    fk_hbm, fv_hbm, fg_hbm, tk_hbm, tv_hbm, tg_hbm, first_ref, count_ref,
    fo_ref, to_ref, fkg_ref, fvg_ref, tkg_ref, tvg_ref,
    frames, tx, win, bias, s_scr, a_scr, b_scr, p_scr, ec_scr, x_low, y_low, fd_scr,
    st, st_m1, st_p1, st_m2, st_p2, fac,
    uvs, uvr, uvo, tks, tkr, tko,
    tx_sem, fl_sem, xl_sem, xs_sem, xr_sem, us_sem, ur_sem, ds_sem, dr_sem,
    ss_sem, sr_sem, uvs_sem, uvr_sem, tks_sem, tkr_sem,
):
    f = lax.axis_index("frame")
    t = lax.axis_index("text")
    rows = tx.shape[1]
    n_frames = frames.shape[1]
    blocks = n_frames // BLOCK
    scale = 1.0 / math.sqrt(D)
    scale2 = scale * math.log2(math.e)
    up1, up2 = lax.rem(f + 1, fdim), lax.rem(f + 2, fdim)
    dn1, dn2 = lax.rem(f + fdim - 1, fdim), lax.rem(f + fdim - 2, fdim)
    own = pl.ds(pl.multiple_of(t * rows, rows), rows)
    has_up, has_up2 = f < fdim - 1, f < fdim - 2
    has_dn, has_dn2 = f > 0, f > 1

    def lanes(i):
        return pl.ds(pl.multiple_of(i * D, D), D)

    def tx_load(a):
        return pltpu.make_async_copy((tk_hbm, tv_hbm, tg_hbm)[a], tx.at[a], tx_sem.at[a])

    def frame_load(a):
        return pltpu.make_async_copy((fk_hbm, fv_hbm, fg_hbm)[a], frames.at[a], fl_sem.at[a])

    def remote(src, dst, send, recv, frame, text):
        return pltpu.make_async_remote_copy(
            src_ref=src, dst_ref=dst, send_sem=send, recv_sem=recv,
            device_id=(frame, text), device_id_type=MESH,
        )

    def x_copy(h, d):
        peer = lax.rem(t + d, tdim)
        return remote(
            tx.at[:, :, lanes(peer * heads + h)], win.at[h, :, 1, own, :],
            xs_sem, xr_sem.at[h, d - 1], f, peer,
        )

    def x_own(h):
        return pltpu.make_async_copy(
            tx.at[:, :, lanes(t * heads + h)], win.at[h, :, 1, own, :], xl_sem.at[h]
        )

    def piece(d):
        return pl.ds(pl.multiple_of(lax.rem(t + tdim - d, tdim) * rows, rows), rows)

    def window(h, d):
        if d is None:
            return (
                remote(win.at[h, :, 1], win.at[h, :, 0], us_sem, ur_sem.at[h], up1, t),
                remote(win.at[h, :, 1], win.at[h, :, 2], ds_sem, dr_sem.at[h], dn1, t),
            )
        at = piece(d)
        src = win.at[h, :, 1, at, :] if d else tx.at[:, :, lanes(t * heads + h)]
        return (
            remote(src, win.at[h, :, 0, at, :], us_sem, ur_sem.at[h], up1, t),
            remote(src, win.at[h, :, 2, at, :], ds_sem, dr_sem.at[h], dn1, t),
        )

    def stats(h):
        a, b = st.at[h, 0], st.at[h, 1]
        return (
            remote(a, st_m1.at[h], ss_sem.at[0], sr_sem.at[h, 0], up1, t),
            remote(b, st_p1.at[h], ss_sem.at[1], sr_sem.at[h, 1], dn1, t),
        )

    def stats2(h):
        a, b = st.at[h, 0], st.at[h, 1]
        return (
            remote(a, st_m2.at[h], ss_sem.at[2], sr_sem.at[h, 2], up2, t),
            remote(b, st_p2.at[h], ss_sem.at[3], sr_sem.at[h, 3], dn2, t),
        )

    def uv_copies(h):
        return (
            remote(uvs.at[h, 1], uvr.at[h, 1], uvs_sem.at[1], uvr_sem.at[h, 1], up1, t),
            remote(uvs.at[h, 0], uvr.at[h, 0], uvs_sem.at[0], uvr_sem.at[h, 0], dn1, t),
        )

    def tk_copies(h):
        return (
            remote(tks.at[h, 1], tkr.at[h, 1], tks_sem.at[1], tkr_sem.at[h, 1], up1, t),
            remote(tks.at[h, 0], tkr.at[h, 0], tks_sem.at[0], tkr_sem.at[h, 0], dn1, t),
        )

    def each(action, ups, downs, *pairs):
        @pl.when(ups)
        def _():
            for pair in pairs:
                getattr(pair[0], action)()

        @pl.when(downs)
        def _():
            for pair in pairs:
                getattr(pair[1], action)()

    def start(*pairs):
        each("start", has_up, has_dn, *pairs)

    def arrived(*pairs):
        each("wait_recv", has_dn, has_up, *pairs)

    def sent(*pairs):
        each("wait_send", has_up, has_dn, *pairs)

    for a in range(3):
        tx_load(a).start()

    barrier = pltpu.get_barrier_semaphore()
    for d in range(1, tdim):
        pl.semaphore_signal(
            barrier, inc=1, device_id=(f, lax.rem(t + d, tdim)), device_id_type=MESH
        )
    for there, frame in ((has_up, up1), (has_dn, dn1), (has_up2, up2), (has_dn2, dn2)):

        @pl.when(there)
        def _():
            pl.semaphore_signal(barrier, inc=1, device_id=(frame, t), device_id_type=MESH)

    for a in range(3):
        frame_load(a).start()

    def blank(tile):
        tile[...] = jnp.ones(tile.shape, F32)
        tile[:, 0:1, :] = jnp.full((heads, 1, BLOCK), FLOOR, F32)
        tile[:, 3:4, :] = jnp.full((heads, 1, BLOCK), FLOOR, F32)

    for there, slot, tile, side in ((has_dn, 0, st_m1, 1), (has_up, 2, st_p1, 0)):

        @pl.when(jnp.logical_not(there))
        def _():
            blank(tile)

            @pl.loop(0, heads)
            def _(h):
                for a in range(3):
                    win[h, a, slot] = jnp.zeros((BLOCK, D), BF16)
                for a in range(2):
                    uvr[h, side, a] = jnp.zeros((D, BLOCK), BF16)
                tkr[h, side] = jnp.zeros((D, BLOCK), BF16)

    for there, tile in ((has_dn2, st_m2), (has_up2, st_p2)):

        @pl.when(jnp.logical_not(there))
        def _():
            blank(tile)

    for b in range(blocks):
        for s in range(3):
            text_id = f - 1 + s
            low = first_ref[b]
            live = (text_id >= low) & (text_id < low + count_ref[b]) & (text_id < fdim)
            bias[b, :, s * BLOCK : (s + 1) * BLOCK] = jnp.full(
                (1, BLOCK), jnp.where(live, 0.0, NEGATIVE), F32
            )

    peers = sum(there.astype(jnp.int32) for there in (has_up, has_dn, has_up2, has_dn2))
    pl.semaphore_wait(barrier, peers + tdim - 1)

    for a in range(3):
        tx_load(a).wait()

    @pl.loop(0, heads)
    def _(h):
        for d in range(1, tdim):
            x_copy(h, d).start()
        start(window(h, 0))
        x_own(h).start()

    def forward(h):
        for d in range(1, tdim):
            x_copy(h, d).wait_recv()
            start(window(h, d))

    def text(h, a):
        return win[h, a].reshape(3 * BLOCK, D)

    def part(b):
        return slice(b * BLOCK, (b + 1) * BLOCK)

    def phase1(h):
        x_own(h).wait()
        arrived(window(h, None))
        s_scr[...] = dot_nt(frames[0, :, lanes(h)], text(h, 0))
        b_scr[h] = dot_nt(frames[1, :, lanes(h)], text(h, 2))
        peak = jnp.full((1, 3 * BLOCK), FLOOR, F32)
        for b in range(blocks):
            s = s_scr[part(b), :] * scale2 + bias[b]
            s_scr[part(b), :] = s
            peak = jnp.maximum(peak, jnp.max(s, axis=0, keepdims=True))
            e = jnp.exp2(s - jnp.max(s, axis=1, keepdims=True))
            p = e * (1.0 / jnp.sum(e, axis=1, keepdims=True))
            p_scr[h, part(b), :] = p
            x_low[part(b), :] = p.astype(BF16)
        total = jnp.zeros((1, 3 * BLOCK), F32)
        dots = jnp.zeros((1, 3 * BLOCK), F32)
        for b in range(blocks):
            e = jnp.exp2(s_scr[part(b), :] - peak)
            ec_scr[h, part(b), :] = e
            y_low[part(b), :] = e.astype(BF16)
            total = total + jnp.sum(e, axis=0, keepdims=True)
            dots = dots + jnp.sum(e * b_scr[h, part(b), :], axis=0, keepdims=True)
        for i, pair in enumerate(((1, 2), (0, 1))):
            for j, slot in enumerate(pair):
                for k, row in enumerate((peak, total, dots)):
                    st[h, i, 3 * j + k : 3 * j + k + 1, :] = row[:, part(slot)]
        start(stats(h))
        each("start", has_up2, has_dn2, stats2(h))
        u = dot_tn(frames[1, :, lanes(h)], y_low[...])
        v = dot_tn(frames[2, :, lanes(h)], x_low[...])
        for i, value in enumerate((u, v)):
            uvs[h, 0, i] = value[:, part(0)].astype(BF16)
            uvo[h, i] = value[:, part(1)]
            uvs[h, 1, i] = value[:, part(2)].astype(BF16)
        start(uv_copies(h))
        out = dot_nn(x_low[...], text(h, 1)).astype(BF16)
        fo_ref[:, lanes(h)] = out
        fd_scr[h] = jnp.sum(
            out.astype(F32) * frames[2, :, lanes(h)].astype(F32), axis=1, keepdims=True
        )

    def phase2(h):
        arrived(stats(h))
        each("wait_recv", has_dn2, has_up2, stats2(h))
        a, b, m1, p1, m2, p2 = st[h, 0], st[h, 1], st_m1[h], st_p1[h], st_m2[h], st_p2[h]
        members = (
            (b[0:3], m1[0:3], m2[3:6]),
            (a[0:3], m1[3:6], p1[0:3]),
            (a[3:6], p1[3:6], p2[0:3]),
        )
        gains, dots = [], []
        for s, tiles in enumerate(members):
            tops = [tile[0:1] for tile in tiles]
            peak = functools.reduce(jnp.maximum, tops)
            factors = [jnp.exp2(top - peak) for top in tops]
            total = sum(tile[1:2] * factor for tile, factor in zip(tiles, factors))
            inverse = 1.0 / total
            dot = sum(tile[2:3] * factor for tile, factor in zip(tiles, factors)) * inverse
            gains.append(factors[0] * inverse)
            dots.append(dot)
            if s == 1:
                for i in range(3):
                    fac[h, i : i + 1, :] = factors[i] * inverse
        gain = jnp.concatenate(gains, axis=1)
        text_dot = jnp.concatenate(dots, axis=1)
        a_scr[...] = dot_nt(frames[2, :, lanes(h)], text(h, 1))
        for b in range(blocks):
            c = ec_scr[h, part(b), :] * gain
            y_low[part(b), :] = c.astype(BF16)
            g = p_scr[h, part(b), :] * (a_scr[part(b), :] - fd_scr[h, part(b), :]) + c * (
                b_scr[h, part(b), :] - text_dot
            )
            x_low[part(b), :] = g.astype(BF16)
        k = dot_tn(frames[0, :, lanes(h)], x_low[...])
        tks[h, 0] = k[:, part(0)].astype(BF16)
        tko[h] = k[:, part(1)]
        tks[h, 1] = k[:, part(2)].astype(BF16)
        start(tk_copies(h))
        fkg_ref[:, lanes(h)] = (scale * dot_nn(x_low[...], text(h, 0))).astype(BF16)
        fvg_ref[:, lanes(h)] = dot_nn(y_low[...], text(h, 2)).astype(BF16)

    def phase3(h):
        arrived(uv_copies(h), tk_copies(h))
        out = (
            uvo[h, 0] * fac[h, 0:1, :]
            + uvr[h, 1, 0].astype(F32) * fac[h, 1:2, :]
            + uvr[h, 0, 0].astype(F32) * fac[h, 2:3, :]
        )
        to_ref[:, lanes(h)] = out.T.astype(BF16)
        keys = scale * (tko[h] + tkr[h, 1].astype(F32) + tkr[h, 0].astype(F32))
        tkg_ref[:, lanes(h)] = keys.T.astype(BF16)
        values = uvo[h, 1] + uvr[h, 1, 1].astype(F32) + uvr[h, 0, 1].astype(F32)
        tvg_ref[:, lanes(h)] = values.T.astype(BF16)

    ahead = min(AHEAD, heads)
    lag = min(LAG, heads)

    @pl.loop(0, ahead)
    def _(h):
        forward(h)

    for a in range(3):
        frame_load(a).wait()

    @pl.loop(0, heads + lag + 1)
    def _(i):
        @pl.when(i < heads)
        def _():
            phase1(i)

        @pl.when(i + ahead < heads)
        def _():
            forward(i + ahead)

        @pl.when((i >= lag) & (i < heads + lag))
        def _():
            phase2(i - lag)

        @pl.when(i >= lag + 1)
        def _():
            phase3(i - lag - 1)

    def total(ref, sem):
        return remote(ref, ref, sem, sem, up1, t)

    total(win.at[:, :, 1, pl.ds(0, (tdim - 1) * rows), :], xs_sem).wait_send()
    sent(
        (total(win.at[:, :, 0], us_sem), total(win.at[:, :, 2], ds_sem)),
        (total(st_m1, ss_sem.at[0]), total(st_p1, ss_sem.at[1])),
        (total(uvr.at[:, 1], uvs_sem.at[1]), total(uvr.at[:, 0], uvs_sem.at[0])),
        (total(tkr.at[:, 1], tks_sem.at[1]), total(tkr.at[:, 0], tks_sem.at[0])),
    )
    each(
        "wait_send", has_up2, has_dn2,
        (total(st_m2, ss_sem.at[2]), total(st_p2, ss_sem.at[3])),
    )


def writer(*refs):
    sources, targets, sem = refs[:6], refs[6:12], refs[12]
    copies = [
        pltpu.make_async_copy(sources[i], targets[i], sem.at[i]) for i in range(6)
    ]
    for copy in copies:
        copy.start()
    for copy in copies:
        copy.wait()


def on_device(fdim, tdim, *args):
    n_frames, width = args[0].shape
    rows = args[3].shape[0]
    heads = width // D
    own_rows = rows * tdim
    window = 3 * BLOCK
    blocks = n_frames // BLOCK
    shape = jax.ShapeDtypeStruct
    frame_out, text_out = shape((n_frames, width), BF16), shape((own_rows, width), BF16)
    dma = pltpu.SemaphoreType.DMA
    vmem = pltpu.VMEM
    hbm_spec = pl.BlockSpec(memory_space=pltpu.HBM)
    vmem_spec = pl.BlockSpec(memory_space=pltpu.VMEM)
    smem_spec = pl.BlockSpec(memory_space=pltpu.SMEM)
    outs = (frame_out, text_out, frame_out, frame_out, text_out, text_out)
    results = pl.pallas_call(
        functools.partial(kernel, fdim, tdim, heads),
        out_shape=tuple(vmem(out.shape, out.dtype) for out in outs),
        in_specs=[hbm_spec] * 6 + [smem_spec] * 2,
        out_specs=(vmem_spec,) * 6,
        scratch_shapes=[
            vmem((3, n_frames, width), BF16),
            vmem((3, rows, args[3].shape[1]), BF16),
            vmem((heads, 3, 3, BLOCK, D), BF16),
            vmem((blocks, 1, window), F32),
            vmem((n_frames, window), F32),
            vmem((n_frames, window), F32),
            vmem((heads, n_frames, window), F32),
            vmem((heads, n_frames, window), F32),
            vmem((heads, n_frames, window), F32),
            vmem((n_frames, window), BF16),
            vmem((n_frames, window), BF16),
            vmem((heads, n_frames, 1), F32),
            vmem((heads, 2, 8, BLOCK), F32),
            vmem((heads, 8, BLOCK), F32),
            vmem((heads, 8, BLOCK), F32),
            vmem((heads, 8, BLOCK), F32),
            vmem((heads, 8, BLOCK), F32),
            vmem((heads, 8, BLOCK), F32),
            vmem((heads, 2, 2, D, BLOCK), BF16),
            vmem((heads, 2, 2, D, BLOCK), BF16),
            vmem((heads, 2, D, BLOCK), F32),
            vmem((heads, 2, D, BLOCK), BF16),
            vmem((heads, 2, D, BLOCK), BF16),
            vmem((heads, D, BLOCK), F32),
            dma((3,)),
            dma((3,)),
            dma((heads,)),
            dma,
            dma((heads, max(tdim - 1, 1))),
            dma,
            dma((heads,)),
            dma,
            dma((heads,)),
            dma((4,)),
            dma((heads, 4)),
            dma((2,)),
            dma((heads, 2)),
            dma((2,)),
            dma((heads, 2)),
        ],
        compiler_params=pltpu.CompilerParams(
            collective_id=0, has_side_effects=True, vmem_limit_bytes=60 << 20
        ),
    )(*args)
    return pl.pallas_call(
        writer,
        out_shape=outs,
        in_specs=[vmem_spec] * 6,
        out_specs=(hbm_spec,) * 6,
        scratch_shapes=[dma((6,))],
        compiler_params=pltpu.CompilerParams(vmem_limit_bytes=1 << 20),
    )(*results)


def solution(mesh):
    whole = P("frame", "text")
    split = P(("frame", "text"), None)
    return jax.shard_map(
        functools.partial(on_device, mesh.shape["frame"], mesh.shape["text"]),
        mesh=mesh,
        in_specs=(whole,) * 3 + (split,) * 3 + (P("frame"),) * 2,
        out_specs=(whole,) * 6,
        check_vma=False,
    )
```

```python
import functools
import math

import jax
import jax.numpy as jnp
from jax import lax
from jax.experimental import pallas as pl
from jax.experimental.pallas import tpu as pltpu
from jax.sharding import PartitionSpec as P

D = 128
BLOCK = 128
NEGATIVE = -1e30
FLOOR = -1e20
LAG = 3
FIRST = 3
HOLD = 5
BULK = 3
MESH = pl.DeviceIdType.MESH
F32 = jnp.float32
BF16 = jnp.bfloat16


def dot_nt(a, b):
    return lax.dot_general(a, b, (((1,), (1,)), ((), ())), preferred_element_type=F32)


def dot_nn(a, b):
    return lax.dot_general(a, b, (((1,), (0,)), ((), ())), preferred_element_type=F32)


def dot_tn(a, b):
    return lax.dot_general(a, b, (((0,), (0,)), ((), ())), preferred_element_type=F32)


def kernel(
    fdim, tdim, heads,
    fk_hbm, fv_hbm, fg_hbm, tk_hbm, tv_hbm, tg_hbm, first_ref, count_ref,
    fo_ref, to_ref, fkg_ref, fvg_ref, tkg_ref, tvg_ref,
    frames, tx, win, bias, s_scr, a_scr, b_scr, p_scr, ec_scr,
    xs_low, ys_low, gs_low, cs_low, turned, fd_scr,
    st, st_m1, st_p1, st_m2, st_p2, fac,
    uvs, uvr, uvo, tks, tkr, tko,
    tx_sem, fl_sem, xl_sem, xs_sem, xr_sem, us_sem, ur_sem, ds_sem, dr_sem,
    ss_sem, sr_sem, uvs_sem, uvr_sem, tks_sem, tkr_sem,
):
    f = lax.axis_index("frame")
    t = lax.axis_index("text")
    rows = tx.shape[1]
    n_frames = frames.shape[1]
    blocks = n_frames // BLOCK
    scale = 1.0 / math.sqrt(D)
    scale2 = scale * math.log2(math.e)
    up1, up2 = lax.rem(f + 1, fdim), lax.rem(f + 2, fdim)
    dn1, dn2 = lax.rem(f + fdim - 1, fdim), lax.rem(f + fdim - 2, fdim)
    own = pl.ds(pl.multiple_of(t * rows, rows), rows)
    has_up, has_up2 = f < fdim - 1, f < fdim - 2
    has_dn, has_dn2 = f > 0, f > 1

    def lanes(i):
        if isinstance(i, int):
            return slice(i * D, (i + 1) * D)
        return pl.ds(pl.multiple_of(i * D, D), D)

    def tx_load(a):
        return pltpu.make_async_copy((tk_hbm, tv_hbm, tg_hbm)[a], tx.at[a], tx_sem.at[a])

    def frame_load(a):
        return pltpu.make_async_copy((fk_hbm, fv_hbm, fg_hbm)[a], frames.at[a], fl_sem.at[a])

    def remote(src, dst, send, recv, frame, text):
        return pltpu.make_async_remote_copy(
            src_ref=src, dst_ref=dst, send_sem=send, recv_sem=recv,
            device_id=(frame, text), device_id_type=MESH,
        )

    def x_copy(h, d):
        peer = lax.rem(t + d, tdim)
        return remote(
            tx.at[:, :, lanes(peer * heads + h)], win.at[h, :, 1, own, :],
            xs_sem, xr_sem.at[h, d - 1], f, peer,
        )

    def x_own(h):
        return pltpu.make_async_copy(
            tx.at[:, :, lanes(t * heads + h)], win.at[h, :, 1, own, :], xl_sem.at[h]
        )

    def piece(d):
        return pl.ds(pl.multiple_of(lax.rem(t + tdim - d, tdim) * rows, rows), rows)

    def window(h, d):
        if d is None:
            return (
                remote(win.at[h, :, 1], win.at[h, :, 0], us_sem, ur_sem.at[h], up1, t),
                remote(win.at[h, :, 1], win.at[h, :, 2], ds_sem, dr_sem.at[h], dn1, t),
            )
        at = piece(d)
        src = win.at[h, :, 1, at, :] if d else tx.at[:, :, lanes(t * heads + h)]
        return (
            remote(src, win.at[h, :, 0, at, :], us_sem, ur_sem.at[h], up1, t),
            remote(src, win.at[h, :, 2, at, :], ds_sem, dr_sem.at[h], dn1, t),
        )

    def stats(h):
        a, b = st.at[h, 0], st.at[h, 1]
        return (
            remote(a, st_m1.at[h], ss_sem.at[0], sr_sem.at[h, 0], up1, t),
            remote(b, st_p1.at[h], ss_sem.at[1], sr_sem.at[h, 1], dn1, t),
        )

    def stats2(h):
        a, b = st.at[h, 0], st.at[h, 1]
        return (
            remote(a, st_m2.at[h], ss_sem.at[2], sr_sem.at[h, 2], up2, t),
            remote(b, st_p2.at[h], ss_sem.at[3], sr_sem.at[h, 3], dn2, t),
        )

    def uv_copies(h):
        return (
            remote(uvs.at[h, 1], uvr.at[h, 1], uvs_sem.at[1], uvr_sem.at[h, 1], up1, t),
            remote(uvs.at[h, 0], uvr.at[h, 0], uvs_sem.at[0], uvr_sem.at[h, 0], dn1, t),
        )

    def tk_copies(h):
        return (
            remote(tks.at[h, 1], tkr.at[h, 1], tks_sem.at[1], tkr_sem.at[h, 1], up1, t),
            remote(tks.at[h, 0], tkr.at[h, 0], tks_sem.at[0], tkr_sem.at[h, 0], dn1, t),
        )

    def act(action, *guarded):
        for there, copies in guarded:

            @pl.when(there)
            def _():
                for copy in copies:
                    getattr(copy, action)()

    def split(pairs):
        return [pair[0] for pair in pairs], [pair[1] for pair in pairs]

    def start(pairs, far=()):
        if not pairs:
            return
        ups, downs = split(pairs)
        act("start", (has_up, ups), (has_dn, downs))
        if far:
            ups, downs = split(far)
            act("start", (has_up2, ups), (has_dn2, downs))

    def arrived(pairs, far=()):
        if not pairs:
            return
        ups, downs = split(pairs)
        act("wait_recv", (has_dn, ups), (has_up, downs))
        if far:
            ups, downs = split(far)
            act("wait_recv", (has_dn2, ups), (has_up2, downs))

    for a in range(3):
        tx_load(a).start()

    barrier = pltpu.get_barrier_semaphore()
    for d in range(1, tdim):
        pl.semaphore_signal(
            barrier, inc=1, device_id=(f, lax.rem(t + d, tdim)), device_id_type=MESH
        )
    for there, frame in ((has_up, up1), (has_dn, dn1), (has_up2, up2), (has_dn2, dn2)):

        @pl.when(there)
        def _():
            pl.semaphore_signal(barrier, inc=1, device_id=(frame, t), device_id_type=MESH)

    for a in range(3):
        frame_load(a).start()

    def blank(tile):
        tile[...] = jnp.ones(tile.shape, F32)
        tile[:, 0:1, :] = jnp.full((heads, 1, BLOCK), FLOOR, F32)
        tile[:, 3:4, :] = jnp.full((heads, 1, BLOCK), FLOOR, F32)

    for there, slot, tile, side in ((has_dn, 0, st_m1, 1), (has_up, 2, st_p1, 0)):

        @pl.when(jnp.logical_not(there))
        def _():
            blank(tile)

            @pl.loop(0, heads)
            def _(h):
                for a in range(3):
                    win[h, a, slot] = jnp.zeros((BLOCK, D), BF16)
                for a in range(2):
                    uvr[h, side, a] = jnp.zeros((D, BLOCK), BF16)
                tkr[h, side] = jnp.zeros((D, BLOCK), BF16)

    for there, tile in ((has_dn2, st_m2), (has_up2, st_p2)):

        @pl.when(jnp.logical_not(there))
        def _():
            blank(tile)

    for b in range(blocks):
        for s in range(3):
            text_id = f - 1 + s
            low = first_ref[b]
            live = (text_id >= low) & (text_id < low + count_ref[b]) & (text_id < fdim)
            bias[b, :, s * BLOCK : (s + 1) * BLOCK] = jnp.full(
                (1, BLOCK), jnp.where(live, 0.0, NEGATIVE), F32
            )

    peers = sum(there.astype(jnp.int32) for there in (has_up, has_dn, has_up2, has_dn2))
    pl.semaphore_wait(barrier, peers + tdim - 1)

    for a in range(3):
        tx_load(a).wait()

    @pl.loop(0, heads)
    def _(h):
        for d in range(1, tdim):
            x_copy(h, d).start()
        start([window(h, 0)])
        x_own(h).start()

    def forward(h):
        for d in range(1, tdim):
            x_copy(h, d).wait_recv()
        start([window(h, d) for d in range(1, tdim)])

    def text(h, a):
        return win[h, a].reshape(3 * BLOCK, D)

    def part(b):
        return slice(b * BLOCK, (b + 1) * BLOCK)

    def softmax(h):
        x_low, y_low = xs_low.at[h % 2], ys_low.at[h % 2]
        s_scr[...] = dot_nt(frames[0, :, lanes(h)], text(h, 0))
        b_scr[h] = dot_nt(frames[1, :, lanes(h)], text(h, 2))
        peak = jnp.full((1, 3 * BLOCK), FLOOR, F32)
        for b in range(blocks):
            s = s_scr[part(b), :] * scale2 + bias[b]
            s_scr[part(b), :] = s
            peak = jnp.maximum(peak, jnp.max(s, axis=0, keepdims=True))
            e = jnp.exp2(s - jnp.max(s, axis=1, keepdims=True))
            p = e * (1.0 / jnp.sum(e, axis=1, keepdims=True))
            p_scr[h, part(b), :] = p
            x_low[part(b), :] = p.astype(BF16)
        total = jnp.zeros((1, 3 * BLOCK), F32)
        dots = jnp.zeros((1, 3 * BLOCK), F32)
        for b in range(blocks):
            e = jnp.exp2(s_scr[part(b), :] - peak)
            ec_scr[h, part(b), :] = e
            y_low[part(b), :] = e.astype(BF16)
            total = total + jnp.sum(e, axis=0, keepdims=True)
            dots = dots + jnp.sum(e * b_scr[h, part(b), :], axis=0, keepdims=True)
        for i, pair in enumerate(((1, 2), (0, 1))):
            for j, slot in enumerate(pair):
                for k, row in enumerate((peak, total, dots)):
                    st[h, i, 3 * j + k : 3 * j + k + 1, :] = row[:, part(slot)]

    def values(h):
        x_low, y_low = xs_low.at[h % 2], ys_low.at[h % 2]
        u = dot_nn(turned[1, h], y_low[...])
        v = dot_nn(turned[2, h], x_low[...])
        for i, value in enumerate((u, v)):
            uvs[h, 0, i] = value[:, part(0)].astype(BF16)
            uvo[h, i] = value[:, part(1)]
            uvs[h, 1, i] = value[:, part(2)].astype(BF16)
        out = dot_nn(x_low[...], text(h, 1)).astype(BF16)
        fo_ref[:, lanes(h)] = out
        fd_scr[h] = jnp.sum(
            out.astype(F32) * frames[2, :, lanes(h)].astype(F32), axis=1, keepdims=True
        )

    def scores_grad(h):
        g_low, c_low = gs_low.at[h % 2], cs_low.at[h % 2]
        a, b, m1, p1, m2, p2 = st[h, 0], st[h, 1], st_m1[h], st_p1[h], st_m2[h], st_p2[h]
        members = (
            (b[0:3], m1[0:3], m2[3:6]),
            (a[0:3], m1[3:6], p1[0:3]),
            (a[3:6], p1[3:6], p2[0:3]),
        )
        gains, dots = [], []
        for s, tiles in enumerate(members):
            tops = [tile[0:1] for tile in tiles]
            peak = functools.reduce(jnp.maximum, tops)
            factors = [jnp.exp2(top - peak) for top in tops]
            total = sum(tile[1:2] * factor for tile, factor in zip(tiles, factors))
            inverse = 1.0 / total
            dot = sum(tile[2:3] * factor for tile, factor in zip(tiles, factors)) * inverse
            gains.append(factors[0] * inverse)
            dots.append(dot)
            if s == 1:
                for i in range(3):
                    fac[h, i : i + 1, :] = factors[i] * inverse
        gain = jnp.concatenate(gains, axis=1)
        text_dot = jnp.concatenate(dots, axis=1)
        a_scr[...] = dot_nt(frames[2, :, lanes(h)], text(h, 1))
        for b in range(blocks):
            c = ec_scr[h, part(b), :] * gain
            c_low[part(b), :] = c.astype(BF16)
            g = p_scr[h, part(b), :] * (a_scr[part(b), :] - fd_scr[h, part(b), :]) + c * (
                b_scr[h, part(b), :] - text_dot
            )
            g_low[part(b), :] = g.astype(BF16)

    def grads(h):
        g_low, c_low = gs_low.at[h % 2], cs_low.at[h % 2]
        k = dot_nn(turned[0, h], g_low[...])
        tks[h, 0] = k[:, part(0)].astype(BF16)
        tko[h] = k[:, part(1)]
        tks[h, 1] = k[:, part(2)].astype(BF16)
        fkg_ref[:, lanes(h)] = (scale * dot_nn(g_low[...], text(h, 0))).astype(BF16)
        fvg_ref[:, lanes(h)] = dot_nn(c_low[...], text(h, 2)).astype(BF16)

    def combine(h):
        out = (
            uvo[h, 0] * fac[h, 0:1, :]
            + uvr[h, 1, 0].astype(F32) * fac[h, 1:2, :]
            + uvr[h, 0, 0].astype(F32) * fac[h, 2:3, :]
        )
        to_ref[:, lanes(h)] = out.T.astype(BF16)
        keys = scale * (tko[h] + tkr[h, 1].astype(F32) + tkr[h, 0].astype(F32))
        tkg_ref[:, lanes(h)] = keys.T.astype(BF16)
        values = uvo[h, 1] + uvr[h, 1, 1].astype(F32) + uvr[h, 0, 1].astype(F32)
        tvg_ref[:, lanes(h)] = values.T.astype(BF16)

    for a in range(3):
        frame_load(a).wait()

    @pl.loop(0, heads)
    def _(h):
        for a in range(3):
            turned[a, h] = frames[a, :, lanes(h)].T

    first = min(FIRST, heads)
    for h in range(first):
        forward(h)

    def within(h, stop=heads):
        return [h] if 0 <= h < stop else []

    sends, pending, i = [], [], 0
    while i < heads + LAG + 1 or pending:
        pending += [(uv_copies, h) for h in within(i - 1)]
        pending += [(tk_copies, h) for h in within(i - LAG - 1, heads - 1)]
        pending += [(tk_copies, h) for h in within(i - LAG) if h == heads - 1]
        count = 0 if i < HOLD else BULK if i < heads else len(pending)
        sends.append(pending[:count])
        pending = pending[count:]
        i += 1
    def body(i):
        now, after, middle = within(i), within(i - 1), within(i - LAG)
        late = within(i - LAG - 1, heads - 1)
        last = [h for h in middle if h == heads - 1]
        for h in now:
            x_own(h).wait()
        arrived(
            [window(h, None) for h in now] + [stats(h) for h in middle],
            [stats2(h) for h in middle],
        )
        for h in late:
            grads(h)
        for h in middle:
            scores_grad(h)
        for h in now:
            softmax(h)
        for h in after:
            values(h)
        for h in last:
            grads(h)
        bulk = sends[i]
        start([stats(h) for h in now] + [c(h) for c, h in bulk], [stats2(h) for h in now])
        if i + first < heads:
            forward(i + first)

    for i in range(len(sends)):
        body(i)

    @pl.loop(0, heads)
    def _(h):
        arrived([uv_copies(h), tk_copies(h)])
        combine(h)

    def total(ref, sem):
        return remote(ref, ref, sem, sem, up1, t)

    total(win.at[:, :, 1, pl.ds(0, (tdim - 1) * rows), :], xs_sem).wait_send()
    act(
        "wait_send",
        (
            has_up,
            [
                total(win.at[:, :, 0], us_sem),
                total(st_m1, ss_sem.at[0]),
                total(uvr.at[:, 1], uvs_sem.at[1]),
                total(tkr.at[:, 1], tks_sem.at[1]),
            ],
        ),
        (
            has_dn,
            [
                total(win.at[:, :, 2], ds_sem),
                total(st_p1, ss_sem.at[1]),
                total(uvr.at[:, 0], uvs_sem.at[0]),
                total(tkr.at[:, 0], tks_sem.at[0]),
            ],
        ),
        (has_up2, [total(st_m2, ss_sem.at[2])]),
        (has_dn2, [total(st_p2, ss_sem.at[3])]),
    )


def writer(*refs):
    sources, targets, sem = refs[:6], refs[6:12], refs[12]
    copies = [
        pltpu.make_async_copy(sources[i], targets[i], sem.at[i]) for i in range(6)
    ]
    for copy in copies:
        copy.start()
    for copy in copies:
        copy.wait()


def on_device(fdim, tdim, *args):
    n_frames, width = args[0].shape
    rows = args[3].shape[0]
    heads = width // D
    own_rows = rows * tdim
    window = 3 * BLOCK
    blocks = n_frames // BLOCK
    shape = jax.ShapeDtypeStruct
    frame_out, text_out = shape((n_frames, width), BF16), shape((own_rows, width), BF16)
    dma = pltpu.SemaphoreType.DMA
    vmem = pltpu.VMEM
    hbm_spec = pl.BlockSpec(memory_space=pltpu.HBM)
    vmem_spec = pl.BlockSpec(memory_space=pltpu.VMEM)
    smem_spec = pl.BlockSpec(memory_space=pltpu.SMEM)
    outs = (frame_out, text_out, frame_out, frame_out, text_out, text_out)
    results = pl.pallas_call(
        functools.partial(kernel, fdim, tdim, heads),
        out_shape=tuple(vmem(out.shape, out.dtype) for out in outs),
        in_specs=[hbm_spec] * 6 + [smem_spec] * 2,
        out_specs=(vmem_spec,) * 6,
        scratch_shapes=[
            vmem((3, n_frames, width), BF16),
            vmem((3, rows, args[3].shape[1]), BF16),
            vmem((heads, 3, 3, BLOCK, D), BF16),
            vmem((blocks, 1, window), F32),
            vmem((n_frames, window), F32),
            vmem((n_frames, window), F32),
            vmem((heads, n_frames, window), F32),
            vmem((heads, n_frames, window), F32),
            vmem((heads, n_frames, window), F32),
            vmem((2, n_frames, window), BF16),
            vmem((2, n_frames, window), BF16),
            vmem((2, n_frames, window), BF16),
            vmem((2, n_frames, window), BF16),
            vmem((3, heads, D, n_frames), BF16),
            vmem((heads, n_frames, 1), F32),
            vmem((heads, 2, 8, BLOCK), F32),
            vmem((heads, 8, BLOCK), F32),
            vmem((heads, 8, BLOCK), F32),
            vmem((heads, 8, BLOCK), F32),
            vmem((heads, 8, BLOCK), F32),
            vmem((heads, 8, BLOCK), F32),
            vmem((heads, 2, 2, D, BLOCK), BF16),
            vmem((heads, 2, 2, D, BLOCK), BF16),
            vmem((heads, 2, D, BLOCK), F32),
            vmem((heads, 2, D, BLOCK), BF16),
            vmem((heads, 2, D, BLOCK), BF16),
            vmem((heads, D, BLOCK), F32),
            dma((3,)),
            dma((3,)),
            dma((heads,)),
            dma,
            dma((heads, max(tdim - 1, 1))),
            dma,
            dma((heads,)),
            dma,
            dma((heads,)),
            dma((4,)),
            dma((heads, 4)),
            dma((2,)),
            dma((heads, 2)),
            dma((2,)),
            dma((heads, 2)),
        ],
        compiler_params=pltpu.CompilerParams(
            collective_id=0, has_side_effects=True, vmem_limit_bytes=60 << 20
        ),
    )(*args)
    return pl.pallas_call(
        writer,
        out_shape=outs,
        in_specs=[vmem_spec] * 6,
        out_specs=(hbm_spec,) * 6,
        scratch_shapes=[dma((6,))],
        compiler_params=pltpu.CompilerParams(vmem_limit_bytes=1 << 20),
    )(*results)


def solution(mesh):
    whole = P("frame", "text")
    split = P(("frame", "text"), None)
    return jax.shard_map(
        functools.partial(on_device, mesh.shape["frame"], mesh.shape["text"]),
        mesh=mesh,
        in_specs=(whole,) * 3 + (split,) * 3 + (P("frame"),) * 2,
        out_specs=(whole,) * 6,
        check_vma=False,
    )
```

```python
import functools
import math

import jax
import jax.numpy as jnp
from jax import lax
from jax.experimental import pallas as pl
from jax.experimental.pallas import tpu as pltpu
from jax.sharding import PartitionSpec as P

D = 128
BLOCK = 128
NEGATIVE = -1e30
FLOOR = -1e20
LAG = 4
FIRST = 5
HOLD = 5
BULK = 3
MESH = pl.DeviceIdType.MESH
F32 = jnp.float32
BF16 = jnp.bfloat16


def dot_nt(a, b):
    return lax.dot_general(a, b, (((1,), (1,)), ((), ())), preferred_element_type=F32)


def dot_nn(a, b):
    return lax.dot_general(a, b, (((1,), (0,)), ((), ())), preferred_element_type=F32)


def dot_tn(a, b):
    return lax.dot_general(a, b, (((0,), (0,)), ((), ())), preferred_element_type=F32)


def kernel(
    fdim, tdim, heads,
    fk_hbm, fv_hbm, fg_hbm, tk_hbm, tv_hbm, tg_hbm, first_ref, count_ref,
    fo_ref, to_ref, fkg_ref, fvg_ref, tkg_ref, tvg_ref,
    frames, tx, win, bias, s_scr, a_scr, b_scr, p_scr, ec_scr,
    xs_low, ys_low, gs_low, cs_low, turned, fd_scr,
    st, st_m1, st_p1, st_m2, st_p2, fac,
    uvs, uvr, uvo, tks, tkr, tko,
    tx_sem, fl_sem, xl_sem, xs_sem, xr_sem, us_sem, ur_sem, ds_sem, dr_sem,
    ss_sem, sr_sem, uvs_sem, uvr_sem, tks_sem, tkr_sem,
):
    f = lax.axis_index("frame")
    t = lax.axis_index("text")
    rows = tx.shape[1]
    n_frames = frames.shape[1]
    blocks = n_frames // BLOCK
    scale = 1.0 / math.sqrt(D)
    scale2 = scale * math.log2(math.e)
    up1, up2 = lax.rem(f + 1, fdim), lax.rem(f + 2, fdim)
    dn1, dn2 = lax.rem(f + fdim - 1, fdim), lax.rem(f + fdim - 2, fdim)
    own = pl.ds(pl.multiple_of(t * rows, rows), rows)
    has_up, has_up2 = f < fdim - 1, f < fdim - 2
    has_dn, has_dn2 = f > 0, f > 1

    def lanes(i):
        if isinstance(i, int):
            return slice(i * D, (i + 1) * D)
        return pl.ds(pl.multiple_of(i * D, D), D)

    def tx_load(a):
        return pltpu.make_async_copy((tk_hbm, tv_hbm, tg_hbm)[a], tx.at[a], tx_sem.at[a])

    def frame_load(a):
        return pltpu.make_async_copy((fk_hbm, fv_hbm, fg_hbm)[a], frames.at[a], fl_sem.at[a])

    def remote(src, dst, send, recv, frame, text):
        return pltpu.make_async_remote_copy(
            src_ref=src, dst_ref=dst, send_sem=send, recv_sem=recv,
            device_id=(frame, text), device_id_type=MESH,
        )

    def x_copy(h, d):
        peer = lax.rem(t + d, tdim)
        return remote(
            tx.at[:, :, lanes(peer * heads + h)], win.at[h, :, 1, own, :],
            xs_sem, xr_sem.at[h, d - 1], f, peer,
        )

    def x_own(h):
        return pltpu.make_async_copy(
            tx.at[:, :, lanes(t * heads + h)], win.at[h, :, 1, own, :], xl_sem.at[h]
        )

    def piece(d):
        return pl.ds(pl.multiple_of(lax.rem(t + tdim - d, tdim) * rows, rows), rows)

    def window(h, d):
        if d is None:
            return (
                remote(win.at[h, :, 1], win.at[h, :, 0], us_sem, ur_sem.at[h], up1, t),
                remote(win.at[h, :, 1], win.at[h, :, 2], ds_sem, dr_sem.at[h], dn1, t),
            )
        at = piece(d)
        src = win.at[h, :, 1, at, :] if d else tx.at[:, :, lanes(t * heads + h)]
        return (
            remote(src, win.at[h, :, 0, at, :], us_sem, ur_sem.at[h], up1, t),
            remote(src, win.at[h, :, 2, at, :], ds_sem, dr_sem.at[h], dn1, t),
        )

    def stats(h):
        a, b = st.at[h, 0], st.at[h, 1]
        return (
            remote(a, st_m1.at[h], ss_sem.at[0], sr_sem.at[h, 0], up1, t),
            remote(b, st_p1.at[h], ss_sem.at[1], sr_sem.at[h, 1], dn1, t),
        )

    def stats2(h):
        a, b = st.at[h, 0], st.at[h, 1]
        return (
            remote(a, st_m2.at[h], ss_sem.at[2], sr_sem.at[h, 2], up2, t),
            remote(b, st_p2.at[h], ss_sem.at[3], sr_sem.at[h, 3], dn2, t),
        )

    def uv_copies(h):
        return (
            remote(uvs.at[h, 1], uvr.at[h, 1], uvs_sem.at[1], uvr_sem.at[h, 1], up1, t),
            remote(uvs.at[h, 0], uvr.at[h, 0], uvs_sem.at[0], uvr_sem.at[h, 0], dn1, t),
        )

    def tk_copies(h):
        return (
            remote(tks.at[h, 1], tkr.at[h, 1], tks_sem.at[1], tkr_sem.at[h, 1], up1, t),
            remote(tks.at[h, 0], tkr.at[h, 0], tks_sem.at[0], tkr_sem.at[h, 0], dn1, t),
        )

    def act(action, *guarded):
        for there, copies in guarded:

            @pl.when(there)
            def _():
                for copy in copies:
                    getattr(copy, action)()

    def split(pairs):
        return [pair[0] for pair in pairs], [pair[1] for pair in pairs]

    def start(pairs, far=()):
        if not pairs:
            return
        ups, downs = split(pairs)
        act("start", (has_up, ups), (has_dn, downs))
        if far:
            ups, downs = split(far)
            act("start", (has_up2, ups), (has_dn2, downs))

    def arrived(pairs, far=()):
        if not pairs:
            return
        ups, downs = split(pairs)
        act("wait_recv", (has_dn, ups), (has_up, downs))
        if far:
            ups, downs = split(far)
            act("wait_recv", (has_dn2, ups), (has_up2, downs))

    for a in range(3):
        tx_load(a).start()

    barrier = pltpu.get_barrier_semaphore()
    for d in range(1, tdim):
        pl.semaphore_signal(
            barrier, inc=1, device_id=(f, lax.rem(t + d, tdim)), device_id_type=MESH
        )
    for there, frame in ((has_up, up1), (has_dn, dn1), (has_up2, up2), (has_dn2, dn2)):

        @pl.when(there)
        def _():
            pl.semaphore_signal(barrier, inc=1, device_id=(frame, t), device_id_type=MESH)

    for a in range(3):
        frame_load(a).start()

    def blank(tile):
        tile[...] = jnp.ones(tile.shape, F32)
        tile[:, 0:1, :] = jnp.full((heads, 1, BLOCK), FLOOR, F32)
        tile[:, 3:4, :] = jnp.full((heads, 1, BLOCK), FLOOR, F32)

    for there, slot, tile, side in ((has_dn, 0, st_m1, 1), (has_up, 2, st_p1, 0)):

        @pl.when(jnp.logical_not(there))
        def _():
            blank(tile)

            @pl.loop(0, heads)
            def _(h):
                for a in range(3):
                    win[h, a, slot] = jnp.zeros((BLOCK, D), BF16)
                for a in range(2):
                    uvr[h, side, a] = jnp.zeros((D, BLOCK), BF16)
                tkr[h, side] = jnp.zeros((D, BLOCK), BF16)

    for there, tile in ((has_dn2, st_m2), (has_up2, st_p2)):

        @pl.when(jnp.logical_not(there))
        def _():
            blank(tile)

    for b in range(blocks):
        for s in range(3):
            text_id = f - 1 + s
            low = first_ref[b]
            live = (text_id >= low) & (text_id < low + count_ref[b]) & (text_id < fdim)
            bias[b, :, s * BLOCK : (s + 1) * BLOCK] = jnp.full(
                (1, BLOCK), jnp.where(live, 0.0, NEGATIVE), F32
            )

    peers = sum(there.astype(jnp.int32) for there in (has_up, has_dn, has_up2, has_dn2))
    pl.semaphore_wait(barrier, peers + tdim - 1)

    for a in range(3):
        tx_load(a).wait()

    @pl.loop(0, heads)
    def _(h):
        for d in range(1, tdim):
            x_copy(h, d).start()
        start([window(h, 0)])
        x_own(h).start()

    def forward(h):
        for d in range(1, tdim):
            x_copy(h, d).wait_recv()
        start([window(h, d) for d in range(1, tdim)])

    def text(h, a):
        return win[h, a].reshape(3 * BLOCK, D)

    def part(b):
        return slice(b * BLOCK, (b + 1) * BLOCK)

    def softmax(h):
        x_low, y_low = xs_low.at[h % 2], ys_low.at[h % 2]
        s_scr[...] = dot_nt(frames[0, :, lanes(h)], text(h, 0))
        b_scr[h] = dot_nt(frames[1, :, lanes(h)], text(h, 2))
        peak = jnp.full((1, 3 * BLOCK), FLOOR, F32)
        for b in range(blocks):
            s = s_scr[part(b), :] * scale2 + bias[b]
            s_scr[part(b), :] = s
            peak = jnp.maximum(peak, jnp.max(s, axis=0, keepdims=True))
            e = jnp.exp2(s - jnp.max(s, axis=1, keepdims=True))
            p = e * (1.0 / jnp.sum(e, axis=1, keepdims=True))
            p_scr[h, part(b), :] = p
            x_low[part(b), :] = p.astype(BF16)
        total = jnp.zeros((1, 3 * BLOCK), F32)
        dots = jnp.zeros((1, 3 * BLOCK), F32)
        for b in range(blocks):
            e = jnp.exp2(s_scr[part(b), :] - peak)
            ec_scr[h, part(b), :] = e
            y_low[part(b), :] = e.astype(BF16)
            total = total + jnp.sum(e, axis=0, keepdims=True)
            dots = dots + jnp.sum(e * b_scr[h, part(b), :], axis=0, keepdims=True)
        for i, pair in enumerate(((1, 2), (0, 1))):
            for j, slot in enumerate(pair):
                for k, row in enumerate((peak, total, dots)):
                    st[h, i, 3 * j + k : 3 * j + k + 1, :] = row[:, part(slot)]

    def values(h):
        x_low, y_low = xs_low.at[h % 2], ys_low.at[h % 2]
        u = dot_nn(turned[1, h], y_low[...])
        v = dot_nn(turned[2, h], x_low[...])
        for i, value in enumerate((u, v)):
            uvs[h, 0, i] = value[:, part(0)].astype(BF16)
            uvo[h, i] = value[:, part(1)]
            uvs[h, 1, i] = value[:, part(2)].astype(BF16)
        out = dot_nn(x_low[...], text(h, 1)).astype(BF16)
        fo_ref[:, lanes(h)] = out
        fd_scr[h] = jnp.sum(
            out.astype(F32) * frames[2, :, lanes(h)].astype(F32), axis=1, keepdims=True
        )

    def scores_grad(h):
        g_low, c_low = gs_low.at[h % 2], cs_low.at[h % 2]
        a, b, m1, p1, m2, p2 = st[h, 0], st[h, 1], st_m1[h], st_p1[h], st_m2[h], st_p2[h]
        members = (
            (b[0:3], m1[0:3], m2[3:6]),
            (a[0:3], m1[3:6], p1[0:3]),
            (a[3:6], p1[3:6], p2[0:3]),
        )
        gains, dots = [], []
        for s, tiles in enumerate(members):
            tops = [tile[0:1] for tile in tiles]
            peak = functools.reduce(jnp.maximum, tops)
            factors = [jnp.exp2(top - peak) for top in tops]
            total = sum(tile[1:2] * factor for tile, factor in zip(tiles, factors))
            inverse = 1.0 / total
            dot = sum(tile[2:3] * factor for tile, factor in zip(tiles, factors)) * inverse
            gains.append(factors[0] * inverse)
            dots.append(dot)
            if s == 1:
                for i in range(3):
                    fac[h, i : i + 1, :] = factors[i] * inverse
        gain = jnp.concatenate(gains, axis=1)
        text_dot = jnp.concatenate(dots, axis=1)
        a_scr[...] = dot_nt(frames[2, :, lanes(h)], text(h, 1))
        for b in range(blocks):
            c = ec_scr[h, part(b), :] * gain
            c_low[part(b), :] = c.astype(BF16)
            g = p_scr[h, part(b), :] * (a_scr[part(b), :] - fd_scr[h, part(b), :]) + c * (
                b_scr[h, part(b), :] - text_dot
            )
            g_low[part(b), :] = g.astype(BF16)

    def grads(h):
        g_low, c_low = gs_low.at[h % 2], cs_low.at[h % 2]
        k = dot_nn(turned[0, h], g_low[...])
        tks[h, 0] = k[:, part(0)].astype(BF16)
        tko[h] = k[:, part(1)]
        tks[h, 1] = k[:, part(2)].astype(BF16)
        fkg_ref[:, lanes(h)] = (scale * dot_nn(g_low[...], text(h, 0))).astype(BF16)
        fvg_ref[:, lanes(h)] = dot_nn(c_low[...], text(h, 2)).astype(BF16)

    def combine(h):
        out = (
            uvo[h, 0] * fac[h, 0:1, :]
            + uvr[h, 1, 0].astype(F32) * fac[h, 1:2, :]
            + uvr[h, 0, 0].astype(F32) * fac[h, 2:3, :]
        )
        to_ref[:, lanes(h)] = out.T.astype(BF16)
        keys = scale * (tko[h] + tkr[h, 1].astype(F32) + tkr[h, 0].astype(F32))
        tkg_ref[:, lanes(h)] = keys.T.astype(BF16)
        values = uvo[h, 1] + uvr[h, 1, 1].astype(F32) + uvr[h, 0, 1].astype(F32)
        tvg_ref[:, lanes(h)] = values.T.astype(BF16)

    for a in range(3):
        frame_load(a).wait()

    @pl.loop(0, heads)
    def _(h):
        for a in range(3):
            turned[a, h] = frames[a, :, lanes(h)].T

    first = min(FIRST, heads)
    for h in range(first):
        forward(h)

    def within(h, stop=heads):
        return [h] if 0 <= h < stop else []

    sends, pending, i = [], [], 0
    while i < heads + LAG + 1 or pending:
        pending += [(uv_copies, h) for h in within(i - 1)]
        pending += [(tk_copies, h) for h in within(i - LAG - 1, heads - 1)]
        pending += [(tk_copies, h) for h in within(i - LAG) if h == heads - 1]
        count = 0 if i < HOLD else BULK if i < heads else len(pending)
        sends.append(pending[:count])
        pending = pending[count:]
        i += 1
    def body(i):
        now, after, middle = within(i), within(i - 1), within(i - LAG)
        late = within(i - LAG - 1, heads - 1)
        last = [h for h in middle if h == heads - 1]
        for h in now:
            x_own(h).wait()
        arrived(
            [window(h, None) for h in now] + [stats(h) for h in middle],
            [stats2(h) for h in middle],
        )
        for h in late:
            grads(h)
        for h in middle:
            scores_grad(h)
        for h in now:
            softmax(h)
        for h in after:
            values(h)
        for h in last:
            grads(h)
        bulk = sends[i]
        start([stats(h) for h in now] + [c(h) for c, h in bulk], [stats2(h) for h in now])
        if i + first < heads:
            forward(i + first)

    for i in range(len(sends)):
        body(i)

    @pl.loop(0, heads)
    def _(h):
        arrived([uv_copies(h), tk_copies(h)])
        combine(h)

    def total(ref, sem):
        return remote(ref, ref, sem, sem, up1, t)

    total(win.at[:, :, 1, pl.ds(0, (tdim - 1) * rows), :], xs_sem).wait_send()
    act(
        "wait_send",
        (
            has_up,
            [
                total(win.at[:, :, 0], us_sem),
                total(st_m1, ss_sem.at[0]),
                total(uvr.at[:, 1], uvs_sem.at[1]),
                total(tkr.at[:, 1], tks_sem.at[1]),
            ],
        ),
        (
            has_dn,
            [
                total(win.at[:, :, 2], ds_sem),
                total(st_p1, ss_sem.at[1]),
                total(uvr.at[:, 0], uvs_sem.at[0]),
                total(tkr.at[:, 0], tks_sem.at[0]),
            ],
        ),
        (has_up2, [total(st_m2, ss_sem.at[2])]),
        (has_dn2, [total(st_p2, ss_sem.at[3])]),
    )


def writer(*refs):
    sources, targets, sem = refs[:6], refs[6:12], refs[12]
    copies = [
        pltpu.make_async_copy(sources[i], targets[i], sem.at[i]) for i in range(6)
    ]
    for copy in copies:
        copy.start()
    for copy in copies:
        copy.wait()


def on_device(fdim, tdim, *args):
    n_frames, width = args[0].shape
    rows = args[3].shape[0]
    heads = width // D
    own_rows = rows * tdim
    window = 3 * BLOCK
    blocks = n_frames // BLOCK
    shape = jax.ShapeDtypeStruct
    frame_out, text_out = shape((n_frames, width), BF16), shape((own_rows, width), BF16)
    dma = pltpu.SemaphoreType.DMA
    vmem = pltpu.VMEM
    hbm_spec = pl.BlockSpec(memory_space=pltpu.HBM)
    vmem_spec = pl.BlockSpec(memory_space=pltpu.VMEM)
    smem_spec = pl.BlockSpec(memory_space=pltpu.SMEM)
    outs = (frame_out, text_out, frame_out, frame_out, text_out, text_out)
    results = pl.pallas_call(
        functools.partial(kernel, fdim, tdim, heads),
        out_shape=tuple(vmem(out.shape, out.dtype) for out in outs),
        in_specs=[hbm_spec] * 6 + [smem_spec] * 2,
        out_specs=(vmem_spec,) * 6,
        scratch_shapes=[
            vmem((3, n_frames, width), BF16),
            vmem((3, rows, args[3].shape[1]), BF16),
            vmem((heads, 3, 3, BLOCK, D), BF16),
            vmem((blocks, 1, window), F32),
            vmem((n_frames, window), F32),
            vmem((n_frames, window), F32),
            vmem((heads, n_frames, window), F32),
            vmem((heads, n_frames, window), F32),
            vmem((heads, n_frames, window), F32),
            vmem((2, n_frames, window), BF16),
            vmem((2, n_frames, window), BF16),
            vmem((2, n_frames, window), BF16),
            vmem((2, n_frames, window), BF16),
            vmem((3, heads, D, n_frames), BF16),
            vmem((heads, n_frames, 1), F32),
            vmem((heads, 2, 8, BLOCK), F32),
            vmem((heads, 8, BLOCK), F32),
            vmem((heads, 8, BLOCK), F32),
            vmem((heads, 8, BLOCK), F32),
            vmem((heads, 8, BLOCK), F32),
            vmem((heads, 8, BLOCK), F32),
            vmem((heads, 2, 2, D, BLOCK), BF16),
            vmem((heads, 2, 2, D, BLOCK), BF16),
            vmem((heads, 2, D, BLOCK), F32),
            vmem((heads, 2, D, BLOCK), BF16),
            vmem((heads, 2, D, BLOCK), BF16),
            vmem((heads, D, BLOCK), F32),
            dma((3,)),
            dma((3,)),
            dma((heads,)),
            dma,
            dma((heads, max(tdim - 1, 1))),
            dma,
            dma((heads,)),
            dma,
            dma((heads,)),
            dma((4,)),
            dma((heads, 4)),
            dma((2,)),
            dma((heads, 2)),
            dma((2,)),
            dma((heads, 2)),
        ],
        compiler_params=pltpu.CompilerParams(
            collective_id=0, has_side_effects=True, vmem_limit_bytes=60 << 20
        ),
    )(*args)
    return pl.pallas_call(
        writer,
        out_shape=outs,
        in_specs=[vmem_spec] * 6,
        out_specs=(hbm_spec,) * 6,
        scratch_shapes=[dma((6,))],
        compiler_params=pltpu.CompilerParams(vmem_limit_bytes=1 << 20),
    )(*results)


def solution(mesh):
    whole = P("frame", "text")
    split = P(("frame", "text"), None)
    return jax.shard_map(
        functools.partial(on_device, mesh.shape["frame"], mesh.shape["text"]),
        mesh=mesh,
        in_specs=(whole,) * 3 + (split,) * 3 + (P("frame"),) * 2,
        out_specs=(whole,) * 6,
        check_vma=False,
    )
```

```python
import functools
import math

import jax
import jax.numpy as jnp
from jax import lax
from jax.experimental import pallas as pl
from jax.experimental.pallas import tpu as pltpu
from jax.sharding import PartitionSpec as P

D = 128
BLOCK = 128
NEGATIVE = -1e30
FLOOR = -1e20
LAG = 4
FIRST = 6
HOLD = 5
BULK = 3
MESH = pl.DeviceIdType.MESH
F32 = jnp.float32
BF16 = jnp.bfloat16


def dot_nt(a, b):
    return lax.dot_general(a, b, (((1,), (1,)), ((), ())), preferred_element_type=F32)


def dot_nn(a, b):
    return lax.dot_general(a, b, (((1,), (0,)), ((), ())), preferred_element_type=F32)


def dot_tn(a, b):
    return lax.dot_general(a, b, (((0,), (0,)), ((), ())), preferred_element_type=F32)


def kernel(
    fdim, tdim, heads,
    fk_hbm, fv_hbm, fg_hbm, tk_hbm, tv_hbm, tg_hbm, first_ref, count_ref,
    fo_ref, to_ref, fkg_ref, fvg_ref, tkg_ref, tvg_ref,
    frames, tx, win, bias, s_scr, a_scr, b_scr, p_scr, ec_scr,
    xs_low, ys_low, gs_low, cs_low, turned, fd_scr,
    st, st_m1, st_p1, st_m2, st_p2, fac,
    uvs, uvr, uvo, tks, tkr, tko,
    tx_sem, fl_sem, xl_sem, xs_sem, xr_sem, us_sem, ur_sem, ds_sem, dr_sem,
    ss_sem, sr_sem, uvs_sem, uvr_sem, tks_sem, tkr_sem,
):
    f = lax.axis_index("frame")
    t = lax.axis_index("text")
    rows = tx.shape[1]
    n_frames = frames.shape[1]
    blocks = n_frames // BLOCK
    scale = 1.0 / math.sqrt(D)
    scale2 = scale * math.log2(math.e)
    up1, up2 = lax.rem(f + 1, fdim), lax.rem(f + 2, fdim)
    dn1, dn2 = lax.rem(f + fdim - 1, fdim), lax.rem(f + fdim - 2, fdim)
    own = pl.ds(pl.multiple_of(t * rows, rows), rows)
    has_up, has_up2 = f < fdim - 1, f < fdim - 2
    has_dn, has_dn2 = f > 0, f > 1

    def lanes(i):
        if isinstance(i, int):
            return slice(i * D, (i + 1) * D)
        return pl.ds(pl.multiple_of(i * D, D), D)

    def tx_load(a):
        return pltpu.make_async_copy((tk_hbm, tv_hbm, tg_hbm)[a], tx.at[a], tx_sem.at[a])

    def frame_load(a):
        return pltpu.make_async_copy((fk_hbm, fv_hbm, fg_hbm)[a], frames.at[a], fl_sem.at[a])

    def remote(src, dst, send, recv, frame, text):
        return pltpu.make_async_remote_copy(
            src_ref=src, dst_ref=dst, send_sem=send, recv_sem=recv,
            device_id=(frame, text), device_id_type=MESH,
        )

    def x_copy(h, d):
        peer = lax.rem(t + d, tdim)
        return remote(
            tx.at[:, :, lanes(peer * heads + h)], win.at[h, :, 1, own, :],
            xs_sem, xr_sem.at[h, d - 1], f, peer,
        )

    def x_own(h):
        return pltpu.make_async_copy(
            tx.at[:, :, lanes(t * heads + h)], win.at[h, :, 1, own, :], xl_sem.at[h]
        )

    def piece(d):
        return pl.ds(pl.multiple_of(lax.rem(t + tdim - d, tdim) * rows, rows), rows)

    def window(h, d):
        if d is None:
            return (
                remote(win.at[h, :, 1], win.at[h, :, 0], us_sem, ur_sem.at[h], up1, t),
                remote(win.at[h, :, 1], win.at[h, :, 2], ds_sem, dr_sem.at[h], dn1, t),
            )
        at = piece(d)
        src = win.at[h, :, 1, at, :] if d else tx.at[:, :, lanes(t * heads + h)]
        return (
            remote(src, win.at[h, :, 0, at, :], us_sem, ur_sem.at[h], up1, t),
            remote(src, win.at[h, :, 2, at, :], ds_sem, dr_sem.at[h], dn1, t),
        )

    def stats(h):
        a, b = st.at[h, 0], st.at[h, 1]
        return (
            remote(a, st_m1.at[h], ss_sem.at[0], sr_sem.at[h, 0], up1, t),
            remote(b, st_p1.at[h], ss_sem.at[1], sr_sem.at[h, 1], dn1, t),
        )

    def stats2(h):
        a, b = st.at[h, 0], st.at[h, 1]
        return (
            remote(a, st_m2.at[h], ss_sem.at[2], sr_sem.at[h, 2], up2, t),
            remote(b, st_p2.at[h], ss_sem.at[3], sr_sem.at[h, 3], dn2, t),
        )

    def uv_copies(h):
        return (
            remote(uvs.at[h, 1], uvr.at[h, 1], uvs_sem.at[1], uvr_sem.at[h, 1], up1, t),
            remote(uvs.at[h, 0], uvr.at[h, 0], uvs_sem.at[0], uvr_sem.at[h, 0], dn1, t),
        )

    def tk_copies(h):
        return (
            remote(tks.at[h, 1], tkr.at[h, 1], tks_sem.at[1], tkr_sem.at[h, 1], up1, t),
            remote(tks.at[h, 0], tkr.at[h, 0], tks_sem.at[0], tkr_sem.at[h, 0], dn1, t),
        )

    def act(action, *guarded):
        for there, copies in guarded:

            @pl.when(there)
            def _():
                for copy in copies:
                    getattr(copy, action)()

    def split(pairs):
        return [pair[0] for pair in pairs], [pair[1] for pair in pairs]

    def start(pairs, far=()):
        if not pairs:
            return
        ups, downs = split(pairs)
        act("start", (has_up, ups), (has_dn, downs))
        if far:
            ups, downs = split(far)
            act("start", (has_up2, ups), (has_dn2, downs))

    def arrived(pairs, far=()):
        if not pairs:
            return
        ups, downs = split(pairs)
        act("wait_recv", (has_dn, ups), (has_up, downs))
        if far:
            ups, downs = split(far)
            act("wait_recv", (has_dn2, ups), (has_up2, downs))

    for a in range(3):
        tx_load(a).start()

    barrier = pltpu.get_barrier_semaphore()
    for d in range(1, tdim):
        pl.semaphore_signal(
            barrier, inc=1, device_id=(f, lax.rem(t + d, tdim)), device_id_type=MESH
        )
    for there, frame in ((has_up, up1), (has_dn, dn1), (has_up2, up2), (has_dn2, dn2)):

        @pl.when(there)
        def _():
            pl.semaphore_signal(barrier, inc=1, device_id=(frame, t), device_id_type=MESH)

    for a in range(3):
        frame_load(a).start()

    def blank(tile):
        tile[...] = jnp.ones(tile.shape, F32)
        tile[:, 0:1, :] = jnp.full((heads, 1, BLOCK), FLOOR, F32)
        tile[:, 3:4, :] = jnp.full((heads, 1, BLOCK), FLOOR, F32)

    for there, slot, tile, side in ((has_dn, 0, st_m1, 1), (has_up, 2, st_p1, 0)):

        @pl.when(jnp.logical_not(there))
        def _():
            blank(tile)

            @pl.loop(0, heads)
            def _(h):
                for a in range(3):
                    win[h, a, slot] = jnp.zeros((BLOCK, D), BF16)
                for a in range(2):
                    uvr[h, side, a] = jnp.zeros((D, BLOCK), BF16)
                tkr[h, side] = jnp.zeros((D, BLOCK), BF16)

    for there, tile in ((has_dn2, st_m2), (has_up2, st_p2)):

        @pl.when(jnp.logical_not(there))
        def _():
            blank(tile)

    for b in range(blocks):
        for s in range(3):
            text_id = f - 1 + s
            low = first_ref[b]
            live = (text_id >= low) & (text_id < low + count_ref[b]) & (text_id < fdim)
            bias[b, :, s * BLOCK : (s + 1) * BLOCK] = jnp.full(
                (1, BLOCK), jnp.where(live, 0.0, NEGATIVE), F32
            )

    peers = sum(there.astype(jnp.int32) for there in (has_up, has_dn, has_up2, has_dn2))
    pl.semaphore_wait(barrier, peers + tdim - 1)

    for a in range(3):
        tx_load(a).wait()

    @pl.loop(0, heads)
    def _(h):
        for d in range(1, tdim):
            x_copy(h, d).start()
        start([window(h, 0)])
        x_own(h).start()

    def forward(h):
        for d in range(1, tdim):
            x_copy(h, d).wait_recv()
        start([window(h, d) for d in range(1, tdim)])

    def text(h, a):
        return win[h, a].reshape(3 * BLOCK, D)

    def part(b):
        return slice(b * BLOCK, (b + 1) * BLOCK)

    def softmax(h):
        x_low, y_low = xs_low.at[h % 2], ys_low.at[h % 2]
        s_scr[...] = dot_nt(frames[0, :, lanes(h)], text(h, 0))
        b_scr[h] = dot_nt(frames[1, :, lanes(h)], text(h, 2))
        peak = jnp.full((1, 3 * BLOCK), FLOOR, F32)
        for b in range(blocks):
            s = s_scr[part(b), :] * scale2 + bias[b]
            s_scr[part(b), :] = s
            peak = jnp.maximum(peak, jnp.max(s, axis=0, keepdims=True))
            e = jnp.exp2(s - jnp.max(s, axis=1, keepdims=True))
            p = e * (1.0 / jnp.sum(e, axis=1, keepdims=True))
            p_scr[h, part(b), :] = p
            x_low[part(b), :] = p.astype(BF16)
        total = jnp.zeros((1, 3 * BLOCK), F32)
        dots = jnp.zeros((1, 3 * BLOCK), F32)
        for b in range(blocks):
            e = jnp.exp2(s_scr[part(b), :] - peak)
            ec_scr[h, part(b), :] = e
            y_low[part(b), :] = e.astype(BF16)
            total = total + jnp.sum(e, axis=0, keepdims=True)
            dots = dots + jnp.sum(e * b_scr[h, part(b), :], axis=0, keepdims=True)
        for i, pair in enumerate(((1, 2), (0, 1))):
            for j, slot in enumerate(pair):
                for k, row in enumerate((peak, total, dots)):
                    st[h, i, 3 * j + k : 3 * j + k + 1, :] = row[:, part(slot)]

    def values(h):
        x_low, y_low = xs_low.at[h % 2], ys_low.at[h % 2]
        u = dot_nn(turned[1, h], y_low[...])
        v = dot_nn(turned[2, h], x_low[...])
        for i, value in enumerate((u, v)):
            uvs[h, 0, i] = value[:, part(0)].astype(BF16)
            uvo[h, i] = value[:, part(1)]
            uvs[h, 1, i] = value[:, part(2)].astype(BF16)
        out = dot_nn(x_low[...], text(h, 1)).astype(BF16)
        fo_ref[:, lanes(h)] = out
        fd_scr[h] = jnp.sum(
            out.astype(F32) * frames[2, :, lanes(h)].astype(F32), axis=1, keepdims=True
        )

    def scores_grad(h):
        g_low, c_low = gs_low.at[h % 2], cs_low.at[h % 2]
        a, b, m1, p1, m2, p2 = st[h, 0], st[h, 1], st_m1[h], st_p1[h], st_m2[h], st_p2[h]
        members = (
            (b[0:3], m1[0:3], m2[3:6]),
            (a[0:3], m1[3:6], p1[0:3]),
            (a[3:6], p1[3:6], p2[0:3]),
        )
        gains, dots = [], []
        for s, tiles in enumerate(members):
            tops = [tile[0:1] for tile in tiles]
            peak = functools.reduce(jnp.maximum, tops)
            factors = [jnp.exp2(top - peak) for top in tops]
            total = sum(tile[1:2] * factor for tile, factor in zip(tiles, factors))
            inverse = 1.0 / total
            dot = sum(tile[2:3] * factor for tile, factor in zip(tiles, factors)) * inverse
            gains.append(factors[0] * inverse)
            dots.append(dot)
            if s == 1:
                for i in range(3):
                    fac[h, i : i + 1, :] = factors[i] * inverse
        gain = jnp.concatenate(gains, axis=1)
        text_dot = jnp.concatenate(dots, axis=1)
        a_scr[...] = dot_nt(frames[2, :, lanes(h)], text(h, 1))
        for b in range(blocks):
            c = ec_scr[h, part(b), :] * gain
            c_low[part(b), :] = c.astype(BF16)
            g = p_scr[h, part(b), :] * (a_scr[part(b), :] - fd_scr[h, part(b), :]) + c * (
                b_scr[h, part(b), :] - text_dot
            )
            g_low[part(b), :] = g.astype(BF16)

    def grads(h):
        g_low, c_low = gs_low.at[h % 2], cs_low.at[h % 2]
        k = dot_nn(turned[0, h], g_low[...])
        tks[h, 0] = k[:, part(0)].astype(BF16)
        tko[h] = k[:, part(1)]
        tks[h, 1] = k[:, part(2)].astype(BF16)
        fkg_ref[:, lanes(h)] = (scale * dot_nn(g_low[...], text(h, 0))).astype(BF16)
        fvg_ref[:, lanes(h)] = dot_nn(c_low[...], text(h, 2)).astype(BF16)

    def combine(h):
        out = (
            uvo[h, 0] * fac[h, 0:1, :]
            + uvr[h, 1, 0].astype(F32) * fac[h, 1:2, :]
            + uvr[h, 0, 0].astype(F32) * fac[h, 2:3, :]
        )
        to_ref[:, lanes(h)] = out.T.astype(BF16)
        keys = scale * (tko[h] + tkr[h, 1].astype(F32) + tkr[h, 0].astype(F32))
        tkg_ref[:, lanes(h)] = keys.T.astype(BF16)
        values = uvo[h, 1] + uvr[h, 1, 1].astype(F32) + uvr[h, 0, 1].astype(F32)
        tvg_ref[:, lanes(h)] = values.T.astype(BF16)

    for a in range(3):
        frame_load(a).wait()

    @pl.loop(0, heads)
    def _(h):
        for a in range(3):
            turned[a, h] = frames[a, :, lanes(h)].T

    first = min(FIRST, heads)
    for h in range(first):
        forward(h)

    def within(h, stop=heads):
        return [h] if 0 <= h < stop else []

    sends, pending, i = [], [], 0
    while i < heads + LAG + 1 or pending:
        pending += [(uv_copies, h) for h in within(i - 1)]
        pending += [(tk_copies, h) for h in within(i - LAG - 1, heads - 1)]
        pending += [(tk_copies, h) for h in within(i - LAG) if h == heads - 1]
        count = 0 if i < HOLD else BULK if i < heads else len(pending)
        sends.append(pending[:count])
        pending = pending[count:]
        i += 1
    def body(i):
        now, after, middle = within(i), within(i - 1), within(i - LAG)
        late = within(i - LAG - 1, heads - 1)
        last = [h for h in middle if h == heads - 1]
        for h in now:
            x_own(h).wait()
        arrived(
            [window(h, None) for h in now] + [stats(h) for h in middle],
            [stats2(h) for h in middle],
        )
        for h in late:
            grads(h)
        for h in middle:
            scores_grad(h)
        for h in now:
            softmax(h)
        for h in after:
            values(h)
        for h in last:
            grads(h)
        bulk = sends[i]
        start([stats(h) for h in now] + [c(h) for c, h in bulk], [stats2(h) for h in now])
        if i + first < heads:
            forward(i + first)

    for i in range(len(sends)):
        body(i)

    @pl.loop(0, heads)
    def _(h):
        arrived([uv_copies(h), tk_copies(h)])
        combine(h)

    def total(ref, sem):
        return remote(ref, ref, sem, sem, up1, t)

    total(win.at[:, :, 1, pl.ds(0, (tdim - 1) * rows), :], xs_sem).wait_send()
    act(
        "wait_send",
        (
            has_up,
            [
                total(win.at[:, :, 0], us_sem),
                total(st_m1, ss_sem.at[0]),
                total(uvr.at[:, 1], uvs_sem.at[1]),
                total(tkr.at[:, 1], tks_sem.at[1]),
            ],
        ),
        (
            has_dn,
            [
                total(win.at[:, :, 2], ds_sem),
                total(st_p1, ss_sem.at[1]),
                total(uvr.at[:, 0], uvs_sem.at[0]),
                total(tkr.at[:, 0], tks_sem.at[0]),
            ],
        ),
        (has_up2, [total(st_m2, ss_sem.at[2])]),
        (has_dn2, [total(st_p2, ss_sem.at[3])]),
    )


def writer(*refs):
    sources, targets, sem = refs[:6], refs[6:12], refs[12]
    copies = [
        pltpu.make_async_copy(sources[i], targets[i], sem.at[i]) for i in range(6)
    ]
    for copy in copies:
        copy.start()
    for copy in copies:
        copy.wait()


def on_device(fdim, tdim, *args):
    n_frames, width = args[0].shape
    rows = args[3].shape[0]
    heads = width // D
    own_rows = rows * tdim
    window = 3 * BLOCK
    blocks = n_frames // BLOCK
    shape = jax.ShapeDtypeStruct
    frame_out, text_out = shape((n_frames, width), BF16), shape((own_rows, width), BF16)
    dma = pltpu.SemaphoreType.DMA
    vmem = pltpu.VMEM
    hbm_spec = pl.BlockSpec(memory_space=pltpu.HBM)
    vmem_spec = pl.BlockSpec(memory_space=pltpu.VMEM)
    smem_spec = pl.BlockSpec(memory_space=pltpu.SMEM)
    outs = (frame_out, text_out, frame_out, frame_out, text_out, text_out)
    results = pl.pallas_call(
        functools.partial(kernel, fdim, tdim, heads),
        out_shape=tuple(vmem(out.shape, out.dtype) for out in outs),
        in_specs=[hbm_spec] * 6 + [smem_spec] * 2,
        out_specs=(vmem_spec,) * 6,
        scratch_shapes=[
            vmem((3, n_frames, width), BF16),
            vmem((3, rows, args[3].shape[1]), BF16),
            vmem((heads, 3, 3, BLOCK, D), BF16),
            vmem((blocks, 1, window), F32),
            vmem((n_frames, window), F32),
            vmem((n_frames, window), F32),
            vmem((heads, n_frames, window), F32),
            vmem((heads, n_frames, window), F32),
            vmem((heads, n_frames, window), F32),
            vmem((2, n_frames, window), BF16),
            vmem((2, n_frames, window), BF16),
            vmem((2, n_frames, window), BF16),
            vmem((2, n_frames, window), BF16),
            vmem((3, heads, D, n_frames), BF16),
            vmem((heads, n_frames, 1), F32),
            vmem((heads, 2, 8, BLOCK), F32),
            vmem((heads, 8, BLOCK), F32),
            vmem((heads, 8, BLOCK), F32),
            vmem((heads, 8, BLOCK), F32),
            vmem((heads, 8, BLOCK), F32),
            vmem((heads, 8, BLOCK), F32),
            vmem((heads, 2, 2, D, BLOCK), BF16),
            vmem((heads, 2, 2, D, BLOCK), BF16),
            vmem((heads, 2, D, BLOCK), F32),
            vmem((heads, 2, D, BLOCK), BF16),
            vmem((heads, 2, D, BLOCK), BF16),
            vmem((heads, D, BLOCK), F32),
            dma((3,)),
            dma((3,)),
            dma((heads,)),
            dma,
            dma((heads, max(tdim - 1, 1))),
            dma,
            dma((heads,)),
            dma,
            dma((heads,)),
            dma((4,)),
            dma((heads, 4)),
            dma((2,)),
            dma((heads, 2)),
            dma((2,)),
            dma((heads, 2)),
        ],
        compiler_params=pltpu.CompilerParams(
            collective_id=0, has_side_effects=True, vmem_limit_bytes=60 << 20
        ),
    )(*args)
    return pl.pallas_call(
        writer,
        out_shape=outs,
        in_specs=[vmem_spec] * 6,
        out_specs=(hbm_spec,) * 6,
        scratch_shapes=[dma((6,))],
        compiler_params=pltpu.CompilerParams(vmem_limit_bytes=1 << 20),
    )(*results)


def solution(mesh):
    whole = P("frame", "text")
    split = P(("frame", "text"), None)
    return jax.shard_map(
        functools.partial(on_device, mesh.shape["frame"], mesh.shape["text"]),
        mesh=mesh,
        in_specs=(whole,) * 3 + (split,) * 3 + (P("frame"),) * 2,
        out_specs=(whole,) * 6,
        check_vma=False,
    )
```
